32 devices in a mesh: design: 8 (over z, x), feat: 4 (over y, core).
Axes of the slice: x: 2, y: 2, z: 4, core: 2. Of those that a mesh axis runs over, the one named last changes fastest.
Arguments:
- table: bfloat16 [32768, 1024], P('design', 'feat'), may hold values from -0.29882812 to 0.29882812
- proj_weight: float32 [1024, 128], P('feat'), may hold values from -0.1875 to 0.1875
- anchor_ids: int32 [4096], P('design'), may hold values from 0 to 32767, as said below
- positive_ids: int32 [4096], P('design'), may hold values from 0 to 32767, as said below
- neg_tiles: int32 [32, 16], P('design'), may hold values from 0 to 255, as said below
Outputs:
- losses: float32 [4096], P('design')
- table_grad: float32 [32768, 1024], P('design', 'feat')
- weight_grad: float32 [1024, 128], P('feat')
The draws below stay inside these ranges and needn't reach their ends.
Inputs may be any that keep to these rules, and one draw needn't show every extreme that they name: `anchor_ids`: entry i lies in the rows held by design index i // 512, that is from that index times 4096 on, 4096 rows. `positive_ids`: entry i lies in the rows held by design index i // 512, that is from that index times 4096 on, 4096 rows. `neg_tiles`: tile t is held by design index t // 32. Among the 4 rows of blocks of one design index, at most 16 entries name tiles held by any one index, and exactly 16 for some index.
All inputs are finite; a program needn't handle non-finite values.
Results may differ from the reference program's by a relative error of at most 0.0004.
Values may be sent and summed in bfloat16 or wider, within the bound.
A program may use at most 192 MiB of HBM per device.

```python
import jax
import jax.numpy as jnp
from jax import lax

D = 1024
P_SIZE = 128
TILE = 128
NEG = 16
TILES_DEV = 32
BLOCKS_DEV = 4
TILES = 256
ROWS = 32768
ANCHOR_BLOCKS = 32
ANCHORS = 4096
N_DESIGN = 8


def owned_rows(key):
    shard_rows = TILES_DEV * TILE
    local_rows = jax.random.randint(key, (N_DESIGN, BLOCKS_DEV * TILE), 0, shard_rows)
    return (local_rows + jnp.arange(N_DESIGN, dtype=jnp.int32)[:, None] * shard_rows).reshape(-1).astype(jnp.int32)


def draw_anchor_ids(key, part):
    return owned_rows(jax.random.fold_in(key, 11))


def draw_positive_ids(key, part):
    return owned_rows(jax.random.fold_in(key, 23))


def draw_neg_tiles(key, part):
    wanted = BLOCKS_DEV * NEG
    capacity = 2 * wanted // N_DESIGN
    slot_count = N_DESIGN * capacity
    key_heat = jax.random.fold_in(key, 31)
    key_noise = jax.random.fold_in(key, 37)
    key_first = jax.random.fold_in(key, 41)
    key_tile = jax.random.fold_in(key, 43)
    key_permute = jax.random.fold_in(key, 47)
    heat = jax.random.randint(key_heat, (N_DESIGN,), 0, 1 << 16)
    noise = jax.random.randint(key_noise, (N_DESIGN, slot_count), 0, 1 << 16)
    slot_index = jnp.arange(slot_count, dtype=jnp.int32)
    slot_owner = slot_index // capacity
    first_owner = jax.random.randint(key_first, (N_DESIGN, 1), 0, N_DESIGN)
    score = (noise + heat[slot_owner][None, :]) * slot_count + slot_index[None, :]
    score = jnp.where(slot_owner[None, :] == first_owner, -1 - slot_index[None, :], score)
    chosen = jnp.argsort(score, axis=1, stable=True)[:, :wanted]
    shuffle = jax.random.permutation(key_permute, wanted)
    chosen = chosen[:, shuffle]
    owner_dev = chosen // capacity
    local_tile = jax.random.randint(key_tile, (N_DESIGN, wanted), 0, TILES_DEV)
    tiles = owner_dev * TILES_DEV + local_tile
    return tiles.reshape(N_DESIGN * BLOCKS_DEV, NEG).astype(jnp.int32)


def level_of(key, shape, cuts, low, largest):
    gain, own = 1.0, jax.random.fold_in(key, 6)
    for position, shards_of in cuts:
        steps = jnp.exp(jax.random.uniform(jax.random.fold_in(own, position), (shards_of,), jnp.float32, low / len(cuts), largest / len(cuts)))
        gain = gain * jnp.repeat(steps, shape[position] // shards_of).reshape([-1 if axis == position else 1 for axis in range(len(shape))])
    return gain


def normal_values(key, shape, deviation, most, pieces=(), kind=jnp.bfloat16):
    array = deviation * jax.random.normal(key, shape, jnp.float32)
    if pieces:
        array = array * level_of(key, shape, pieces, -0.22, 0.18)
    return jnp.clip(array, -most, most).astype(kind)


def setup_inputs(seed: int = 0) -> dict:
    key_of = jax.random.split(jax.random.key(seed), 6)
    table = normal_values(key_of[0], (ROWS, D), 0.05, 0.29882812, ((0, 8), (1, 4)))
    proj_weight = normal_values(key_of[1], (D, P_SIZE), D ** -0.5, 0.1875, ((0, 4),), jnp.float32)
    anchor_ids = draw_anchor_ids(jax.random.fold_in(key_of[5], 71), 0)
    positive_ids = draw_positive_ids(jax.random.fold_in(key_of[5], 71), 0)
    neg_tiles = draw_neg_tiles(jax.random.fold_in(key_of[5], 71), 0)
    return dict(table=table, proj_weight=proj_weight, anchor_ids=anchor_ids, positive_ids=positive_ids, neg_tiles=neg_tiles)


SOFTMAX_TEMP = 0.07
EPSILON = 1e-06

def unit_rows(values):
    return values / jnp.sqrt(lax.optimization_barrier(jnp.sum(values * values, axis=-1, keepdims=True)) + EPSILON)

def block_losses(anchor_z, positive_z, negative_z):
    anchor_unit_vector = unit_rows(anchor_z)
    positive_unit_vector = unit_rows(positive_z)
    negative_unit_vector = unit_rows(negative_z)
    positive_similarity = lax.optimization_barrier(jnp.sum(anchor_unit_vector * positive_unit_vector, axis=-1)) / SOFTMAX_TEMP
    negative_similarity = jnp.einsum('kjc,koc->kjo', anchor_unit_vector, negative_unit_vector, precision=lax.Precision.HIGHEST) / SOFTMAX_TEMP
    total = jnp.exp(positive_similarity) + lax.optimization_barrier(jnp.sum(jnp.exp(negative_similarity), axis=-1))
    return jnp.log(total) - positive_similarity

def reference(table, proj_weight, anchor_ids, positive_ids, neg_tiles):
    embed = table.astype(jnp.float32)
    codes = jnp.dot(embed, proj_weight, precision=lax.Precision.HIGHEST, preferred_element_type=jnp.float32)

    def all_losses(codes_in):
        anchor_z = codes_in[anchor_ids].reshape(ANCHOR_BLOCKS, TILE, P_SIZE)
        positive_z = codes_in[positive_ids].reshape(ANCHOR_BLOCKS, TILE, P_SIZE)
        tiled = codes_in.reshape(TILES, TILE, P_SIZE)
        negative_z = tiled[neg_tiles].reshape(ANCHOR_BLOCKS, NEG * TILE, P_SIZE)
        return block_losses(anchor_z, positive_z, negative_z).reshape(ANCHORS)
    losses, pullback = jax.vjp(all_losses, codes)
    code_grad = pullback(jnp.ones_like(losses))[0]
    table_grad = jnp.dot(code_grad, proj_weight.T, precision=lax.Precision.HIGHEST, preferred_element_type=jnp.float32)
    weight_grad = jnp.dot(embed.T, code_grad, precision=lax.Precision.HIGHEST, preferred_element_type=jnp.float32)
    return (losses, table_grad, weight_grad)
```

```python
import functools

import jax
import jax.numpy as jnp
from jax import lax
from jax.experimental import pallas as pl
from jax.experimental.pallas import tpu as pltpu
from jax.sharding import PartitionSpec as P

TILE = 128
SCALE = 1.0 / 0.07
EPSILON = 1e-06
F32 = jnp.float32
BF16 = jnp.bfloat16
VM = pl.BlockSpec(memory_space=pltpu.VMEM)
SM = pl.BlockSpec(memory_space=pltpu.SMEM)
BIG = pltpu.CompilerParams(vmem_limit_bytes=56 * 1024 * 1024)


def split(v):
    hi = v.astype(BF16)
    return hi, (v - hi.astype(F32)).astype(BF16)


def dot(a, b, ca=1, cb=0):
    return lax.dot_general(a, b, (((ca,), (cb,)), ((), ())), preferred_element_type=F32)


def radius(z):
    return jnp.sqrt(jnp.sum(z * z, axis=-1, keepdims=True) + EPSILON)


def project_kernel(feats, own, aid_ref, pid_ref, table_ref, w_ref, out_ref):
    chunk = table_ref.shape[0] // feats
    stride = chunk + 2 * own
    hi, lo = split(w_ref[...])
    w2 = jnp.concatenate([hi, lo], axis=1)
    width = w_ref.shape[1]
    for c in range(feats):
        both = dot(table_ref[c * chunk : (c + 1) * chunk, :], w2)
        out_ref[c * stride : c * stride + chunk, :] = both[:, :width] + both[:, width:]
    for ids, at in ((aid_ref, chunk), (pid_ref, chunk + own)):
        for c in range(feats):

            def take(i, _):
                for k in range(8):
                    j = i * 8 + k
                    row = ids[c * own + j]
                    source = row + (row // chunk) * (2 * own)
                    out_ref[pl.ds(c * stride + at + j, 1), :] = out_ref[pl.ds(source, 1), :]
                return 0

            lax.fori_loop(0, own // 8, take, 0)


def list_pairs(tiles_ref, first_ref, pairs, mine, negs):
    first = first_ref[0]

    def scan(i, count):
        for k in range(8):
            t = tiles_ref[i * 8 + k] - first
            pairs[count] = ((i * 8 + k) // negs) * mine + t
            count = count + ((t >= 0) & (t < mine)).astype(jnp.int32)
        return count

    return lax.fori_loop(0, tiles_ref.shape[0] // 8, scan, 0)


def similar_t(n_ref, a_hi, a_lo, row):
    nh = n_ref[0, pl.ds(row, TILE), :]
    nl = n_ref[1, pl.ds(row, TILE), :]
    left = jnp.concatenate([nh, nl, nh], axis=1)
    right = jnp.concatenate([a_hi, a_hi, a_lo], axis=1)
    return jnp.exp(dot(left, right, 1, 1) * SCALE)


def forward_kernel(negs, tiles_ref, first_ref, a_ref, z_ref, u_ref, n_ref, pairs):
    mine = z_ref.shape[0] // TILE
    z = z_ref[...]
    unit = z / radius(z)
    n_ref[0], n_ref[1] = split(unit)
    u_ref[...] = jnp.zeros_like(u_ref)
    count = list_pairs(tiles_ref, first_ref, pairs, mine, negs)

    def pair(i, _):
        code = pairs[i]
        b = code // mine
        row = pl.multiple_of((code - b * mine) * TILE, TILE)
        a_hi, a_lo = split(a_ref[b])
        e = similar_t(n_ref, a_hi, a_lo, row)
        u_ref[b, TILE : TILE + 1, :] += jnp.sum(e, axis=0, keepdims=True)
        eh, el = split(e.T)
        nh = n_ref[0, pl.ds(row, TILE), :]
        nl = n_ref[1, pl.ds(row, TILE), :]
        u_ref[b, :TILE, :] += dot(
            jnp.concatenate([eh, el, eh], axis=1), jnp.concatenate([nh, nh, nl], axis=0)
        )
        return 0

    lax.fori_loop(0, count, pair, 0)

    def project(b, _):
        a = a_ref[b]
        u = u_ref[b, :TILE, :]
        u_ref[b, :TILE, :] = u - jnp.sum(u * a, axis=-1, keepdims=True) * a
        return 0

    lax.fori_loop(0, a_ref.shape[0], project, 0)


def backward_kernel(negs, tiles_ref, first_ref, a_ref, z_ref, inv_ref, out_ref, n_ref, acc, pairs):
    mine = z_ref.shape[0] // TILE
    z = z_ref[...]
    r = radius(z)
    unit = z / r
    n_ref[0], n_ref[1] = split(unit)
    acc[...] = jnp.zeros_like(acc)
    count = list_pairs(tiles_ref, first_ref, pairs, mine, negs)

    def pair(i, _):
        code = pairs[i]
        b = code // mine
        row = pl.multiple_of((code - b * mine) * TILE, TILE)
        a_hi, a_lo = split(a_ref[b])
        p = similar_t(n_ref, a_hi, a_lo, row) * inv_ref[pl.ds(b, 1), :]
        ph, pll = split(p)
        acc[pl.ds(row, TILE), :] += dot(
            jnp.concatenate([ph, pll, ph], axis=1), jnp.concatenate([a_hi, a_hi, a_lo], axis=0)
        )
        return 0

    lax.fori_loop(0, count, pair, 0)
    g = acc[...]
    g = (g - jnp.sum(g * unit, axis=-1, keepdims=True) * unit) * (SCALE / r)
    out_ref[...] = g.astype(BF16)


def final_kernel(feats, own, aid_ref, pid_ref, table_ref, w_ref, dn_ref, g_ref, tg_ref, wg_ref, cg):
    rows = table_ref.shape[0]
    width = w_ref.shape[1]
    cg[...] = dn_ref[...].astype(F32)
    for ids, at in ((aid_ref, 0), (pid_ref, own)):
        for c in range(feats):

            def put(i, _):
                for k in range(8):
                    j = i * 8 + k
                    row = ids[c * own + j]
                    cg[pl.ds(row, 1), :] += g_ref[pl.ds(c * 2 * own + at + j, 1), :]
                return 0

            lax.fori_loop(0, own // 8, put, 0)
    wh, wl = split(w_ref[...])
    w3 = jnp.concatenate([wh, wh, wl], axis=1)
    chunk = rows // feats
    total = jnp.zeros((table_ref.shape[1], 2 * width), F32)
    for c in range(feats):
        ch, cl = split(cg[c * chunk : (c + 1) * chunk, :])
        tg_ref[c * chunk : (c + 1) * chunk, :] = dot(jnp.concatenate([ch, cl, ch], axis=1), w3, 1, 1)
        total += dot(
            table_ref[c * chunk : (c + 1) * chunk, :], jnp.concatenate([ch, cl], axis=1), 0, 0
        )
    wg_ref[...] = total[:, :width] + total[:, width:]


def call(kernel, out, args, smem, scratch=()):
    return pl.pallas_call(
        kernel,
        out_shape=out,
        in_specs=[SM if i < smem else VM for i in range(len(args))],
        out_specs=jax.tree.map(lambda _: VM, out),
        scratch_shapes=list(scratch),
        compiler_params=BIG,
    )(*args)


def shards(table, proj_weight, anchor_ids, positive_ids, neg_tiles):
    feats = lax.axis_size("feat")
    design = lax.axis_index("design")
    feat = lax.axis_index("feat")
    both = ("design", "feat")
    rows, depth = table.shape
    width = proj_weight.shape[1]
    blocks, negs = neg_tiles.shape
    own = blocks * TILE // feats
    chunk = rows // feats
    mine = chunk // TILE
    stride = chunk + 2 * own
    shape = jax.ShapeDtypeStruct
    aid = anchor_ids - design * rows
    pid = positive_ids - design * rows
    tiles = lax.all_gather(neg_tiles, "design", tiled=True).reshape(-1)
    first = ((design * feats + feat) * mine).astype(jnp.int32).reshape(1)

    part = call(
        functools.partial(project_kernel, feats, own),
        shape((feats * stride, width), F32),
        (aid, pid, table, proj_weight),
        2,
    )
    mine_z = lax.psum_scatter(part, "feat", scatter_dimension=0, tiled=True)
    z, za, zp = mine_z[:chunk], mine_z[chunk : chunk + own], mine_z[chunk + own :]
    ra, rp = radius(za), radius(zp)
    a, p = za / ra, zp / rp
    every = lax.all_gather(a, both, tiled=True).reshape(-1, TILE, width)
    count = every.shape[0]
    pair_cap = tiles.shape[0] + 8
    u = call(
        functools.partial(forward_kernel, negs),
        shape((count, TILE + 8, width), F32),
        (tiles, first, every, z),
        2,
        (pltpu.VMEM((2, chunk, width), BF16), pltpu.SMEM((pair_cap,), jnp.int32)),
    )
    u = lax.psum_scatter(u, both, scatter_dimension=0, tiled=True)
    s = u[:, TILE, :].reshape(own)
    u = u[:, :TILE, :].reshape(own, width)
    dots = jnp.sum(a * p, axis=-1)
    pos = dots * SCALE
    total = jnp.exp(pos) + s
    losses = jnp.log(total) - pos
    inv = (1.0 / total).reshape(own // TILE, TILE)
    rest = (s / total)[:, None]
    ga = (u / total[:, None] - rest * (p - dots[:, None] * a)) * (SCALE / ra)
    gp = rest * (dots[:, None] * p - a) * (SCALE / rp)
    grads = lax.all_gather(jnp.concatenate([ga, gp], axis=0), "feat", tiled=True)
    losses = lax.all_gather(losses, "feat", tiled=True)
    invs = lax.all_gather(inv, both, tiled=True)
    dn = call(
        functools.partial(backward_kernel, negs),
        shape((chunk, width), BF16),
        (tiles, first, every, z, invs),
        2,
        (
            pltpu.VMEM((2, chunk, width), BF16),
            pltpu.VMEM((chunk, width), F32),
            pltpu.SMEM((pair_cap,), jnp.int32),
        ),
    )
    dn = lax.all_gather(dn, "feat", tiled=True)
    table_grad, weight_part = call(
        functools.partial(final_kernel, feats, own),
        (shape((rows, depth), F32), shape((depth, width), F32)),
        (aid, pid, table, proj_weight, dn, grads),
        2,
        (pltpu.VMEM((rows, width), F32),),
    )
    weight_grad = lax.psum(weight_part, "design")
    return losses, table_grad, weight_grad


def solution(mesh):
    in_specs = (P("design", "feat"), P("feat", None), P("design"), P("design"), P("design", None))
    out_specs = (P("design"), P("design", "feat"), P("feat", None))
    return jax.shard_map(shards, mesh=mesh, in_specs=in_specs, out_specs=out_specs, check_vma=False)
```
